32 devices in a mesh: fsdp: 8 (over z, y), ctx: 4 (over x, core).
Axes of the slice: x: 2, y: 2, z: 4, core: 2. Of those that a mesh axis runs over, the one named last changes fastest.
Arguments:
- tokens: bfloat16 [16384, 1600], P(('fsdp', 'ctx')), may hold values from -6 to 6
- segments: int32 [8, 2048], P('fsdp', 'ctx'), may hold values from 0 to 1, as said below
- ln_gains: bfloat16 [1600, 2], P('fsdp'), may hold values from 0.5 to 1.5
- shifts: bfloat16 [1600, 6], P('fsdp'), may hold values from -3 to 3
- w_qkv: bfloat16 [1600, 4800], P('fsdp'), may hold values from -0.15625 to 0.15625
- w_proj: bfloat16 [1600, 1600], P('fsdp'), may hold values from -0.625 to 0.625
- w_fc: bfloat16 [1600, 6400], P('fsdp'), may hold values from -0.15625 to 0.15625
- fc_bias: bfloat16 [6400], P('fsdp'), may hold values from -3 to 3
- w_out: bfloat16 [6400, 1600], P('fsdp'), may hold values from -0.078125 to 0.078125
- cotangent: bfloat16 [16384, 1600], P(('fsdp', 'ctx')), may hold values from -6 to 6
Outputs:
- result: float32 [16384, 1600], P(('fsdp', 'ctx'))
- grad_tokens: float32 [16384, 1600], P(('fsdp', 'ctx'))
- grad_gains: float32 [1600, 2], P('fsdp')
- grad_shifts: float32 [1600, 6], P('fsdp')
- grad_qkv: float32 [1600, 4800], P('fsdp')
- grad_proj: float32 [1600, 1600], P('fsdp')
- grad_fc: float32 [1600, 6400], P('fsdp')
- grad_fc_bias: float32 [6400], P('fsdp')
- grad_out: float32 [6400, 1600], P('fsdp')
The draws below stay inside these ranges and needn't reach their ends.
Inputs may be any that keep to these rules, and one draw needn't show every extreme that they name: `segments`: each pack holds id 0 on its first positions and id 1 on the rest; each of the two sequences covers 2048 // 4 to 1536 positions; some pack has a sequence of exactly 1536 and some of exactly 512.
All inputs are finite; a program needn't handle non-finite values.
Results may differ from the reference program's by a relative error of at most 0.018.
Values may be sent and summed in bfloat16 or wider, within the bound.
No kernel may reach another device: no remote copies, remote signals or barrier semaphores. Data moves between devices by JAX's collectives and lax.ppermute only.
A program may use at most 384 MiB of HBM per device.

```python
import math
import jax
import jax.numpy as jnp
from jax import lax

D = 1600
HEADS = 25
HEAD_DIM = 64
FF = 6400
GROUP = 2048
SEG_MOST = 1536
TOKENS = 16384


def draw_segments(key, part):
    pack_count = TOKENS // GROUP
    key_len = jax.random.fold_in(key, 11)
    key_perm = jax.random.fold_in(key, 12)
    key_flip = jax.random.fold_in(key, 13)
    first_len = jax.random.randint(key_len, (pack_count,), GROUP // 4, SEG_MOST + 1, dtype=jnp.int32)
    order = jax.random.permutation(key_perm, pack_count)
    pack_index = jnp.arange(pack_count, dtype=jnp.int32)
    first_len = jnp.where(pack_index == order[0], SEG_MOST, first_len)
    first_len = jnp.where(pack_index == order[1], GROUP // 4, first_len)
    flips = jax.random.randint(key_flip, (pack_count,), 0, 2, dtype=jnp.int32)
    first_len = jnp.where(flips == 1, GROUP - first_len, first_len)
    positions = jnp.arange(GROUP, dtype=jnp.int32)
    return (positions[None, :] >= first_len[:, None]).astype(jnp.int32)


def block_levels(stream_key, shape, cuts, low, top_value):
    factor_of = 1.0
    for dim, blocks in cuts:
        heights = jax.random.uniform(jax.random.fold_in(jax.random.fold_in(stream_key, 6), dim), (blocks,), jnp.float32, low / len(cuts), top_value / len(cuts))
        factor_of = factor_of * jnp.repeat(jnp.exp(heights), shape[dim] // blocks).reshape((-1,) + (1,) * (len(shape) - 1 - dim))
    return factor_of


def gaussian(key, extent, scale, most, shards=(), kind=jnp.bfloat16):
    level = block_levels(key, extent, shards, -0.22, 0.18) if shards else 1.0
    drawn = jax.random.normal(key, extent, jnp.float32) * scale * level
    return jnp.minimum(jnp.maximum(drawn, -most), most).astype(kind)


def setup_inputs(seed: int = 0) -> dict:
    streams_of = jax.random.split(jax.random.key(seed), 11)
    tokens = gaussian(streams_of[0], (TOKENS, D), 1.0, 6.0, ((0, 32),))
    segments = draw_segments(jax.random.fold_in(streams_of[10], 71), 0)
    ln_gains = jnp.clip(1.0 + 0.1 * jax.random.normal(streams_of[2], (D, 2), jnp.float32), 0.5, 1.5).astype(jnp.bfloat16)
    shifts = gaussian(streams_of[3], (D, 6), 0.5, 3.0, ((0, 8),))
    w_qkv = gaussian(streams_of[4], (D, 3 * D), D ** -0.5, 0.15625, ((0, 8),))
    w_proj = gaussian(streams_of[5], (D, D), (D // 16) ** -0.5, 0.625, ((0, 8),))
    w_fc = gaussian(streams_of[6], (D, FF), D ** -0.5, 0.15625, ((0, 8),))
    fc_bias = gaussian(streams_of[7], (FF,), 0.5, 3.0, ((0, 8),))
    w_out = gaussian(streams_of[8], (FF, D), FF ** -0.5, 0.078125, ((0, 8),))
    cotangent = gaussian(streams_of[9], (TOKENS, D), 1.0, 6.0, ((0, 32),))
    return {"tokens": tokens, "segments": segments, "ln_gains": ln_gains, "shifts": shifts, "w_qkv": w_qkv, "w_proj": w_proj, "w_fc": w_fc, "fc_bias": fc_bias, "w_out": w_out, "cotangent": cotangent}


@jax.custom_vjp
def low(v):
    return lax.optimization_barrier(v.astype(jnp.bfloat16)).astype(jnp.float32)

@jax.custom_vjp
def low_back(v):
    return v

def low_keep(v):
    return (low(v), None)

def low_pass(kept, grad):
    return (grad,)

def back_keep(v):
    return (v, None)

def back_low(kept, grad):
    return (low(grad),)
low.defvjp(low_keep, low_pass)
low_back.defvjp(back_keep, back_low)
EPS = 1e-05
MASKED = -1e+30

def layer_norm(values, gain_vec, shift_vec):
    row_mean = lax.optimization_barrier(jnp.mean(values, axis=-1, keepdims=True))
    centred = values - row_mean
    spread = lax.optimization_barrier(jnp.mean(centred * centred, axis=-1, keepdims=True))
    return centred * lax.rsqrt(spread + EPS) * gain_vec + shift_vec

def gelu_tanh(values):
    return 0.5 * values * (1.0 + jnp.tanh(0.7978845608028654 * (values + 0.044715 * values * values * values)))

def product(left_side, right_side):
    return jnp.dot(left_side, right_side, precision=lax.Precision.HIGHEST)

def attend(query_rows, key_rows, value_rows, seg_ids):
    group_len = query_rows.shape[0]
    block_len = min(512, group_len)
    block_count = group_len // block_len
    query_heads = query_rows.reshape(block_count, block_len, HEADS, HEAD_DIM)
    key_heads = key_rows.reshape(group_len, HEADS, HEAD_DIM)
    value_heads = value_rows.reshape(group_len, HEADS, HEAD_DIM)
    key_pos = jnp.arange(group_len, dtype=jnp.int32)
    score_scale = 1.0 / math.sqrt(HEAD_DIM)

    def one_block(item):
        query_block, block_index = item
        first_row = block_index * block_len
        query_pos = first_row + jnp.arange(block_len, dtype=jnp.int32)
        query_segs = lax.dynamic_slice_in_dim(seg_ids, first_row, block_len)
        allowed = (query_segs[:, None] == seg_ids[None, :]) & (key_pos[None, :] <= query_pos[:, None])
        scores = low_back(jnp.einsum('qhd,khd->hqk', query_block, key_heads, precision=lax.Precision.HIGHEST) * score_scale)
        scores = jnp.where(allowed[None], scores, MASKED)
        row_top = lax.optimization_barrier(jnp.max(scores, axis=-1, keepdims=True))
        expo_vals = jnp.exp(scores - row_top)
        probs = low(expo_vals / lax.optimization_barrier(jnp.sum(expo_vals, axis=-1, keepdims=True)))
        outputs = jnp.einsum('hqk,khd->qhd', probs, value_heads, precision=lax.Precision.HIGHEST)
        return outputs.reshape(block_len, HEADS * HEAD_DIM)
    blocks_out = lax.map(jax.checkpoint(one_block), (query_heads, jnp.arange(block_count, dtype=jnp.int32)))
    return blocks_out.reshape(group_len, HEADS * HEAD_DIM)

def forward(block_in, seg_ids, gains, biases, w_qkv, w_proj, w_fc, fc_bias, w_out):
    normed = low(layer_norm(block_in, gains[:, 0], biases[:, 0]))
    packed = product(normed, w_qkv)
    query_rows = low(low_back(packed[:, :D] + biases[:, 1]))
    key_rows = low(low_back(packed[:, D:2 * D]))
    value_rows = low(low_back(packed[:, 2 * D:] + biases[:, 2]))
    mixed_rows = low(low_back(attend(query_rows, key_rows, value_rows, seg_ids)))
    hidden = block_in + low_back(product(mixed_rows, w_proj) + biases[:, 3])
    normed_two = low(layer_norm(hidden, gains[:, 1], biases[:, 4]))
    pre_act = low_back(product(normed_two, w_fc) + fc_bias)
    active = low(gelu_tanh(pre_act))
    return hidden + low_back(product(active, w_out) + biases[:, 5])

def reference(tokens, segments, ln_gains, shifts, w_qkv, w_proj, w_fc, fc_bias, w_out, cotangent):
    params = (ln_gains.astype(jnp.float32), shifts.astype(jnp.float32), w_qkv.astype(jnp.float32), w_proj.astype(jnp.float32), w_fc.astype(jnp.float32), fc_bias.astype(jnp.float32), w_out.astype(jnp.float32))
    group_len = segments.shape[1]
    packs_in = tokens.astype(jnp.float32).reshape(-1, group_len, D)
    packs_cot = cotangent.astype(jnp.float32).reshape(-1, group_len, D)

    def one_pack(totals, item):
        pack_in, seg_ids, pack_cot = item

        def apply_block(block_in, gains, biases, wqkv, wproj, wfc, bfc, wout):
            return forward(block_in, seg_ids, gains, biases, wqkv, wproj, wfc, bfc, wout)
        outputs, pullback = jax.vjp(apply_block, pack_in, *params)
        grads = pullback(pack_cot)
        new_totals = tuple((old + new for old, new in zip(totals, grads[1:])))
        return (new_totals, (outputs, grads[0]))
    zeros = tuple((jnp.zeros_like(item) for item in params))
    totals, (outputs, grad_in) = lax.scan(one_pack, zeros, (packs_in, segments, packs_cot))
    grad_gains, grad_shifts, grad_qkv, grad_proj, grad_fc, grad_fc_bias, grad_out = totals
    return (outputs.reshape(-1, D), grad_in.reshape(-1, D), grad_gains, grad_shifts, grad_qkv, grad_proj, grad_fc, grad_fc_bias, grad_out)
```

```python
import functools
import math

import jax
import jax.numpy as jnp
from jax import lax
from jax.experimental import pallas as pl
from jax.experimental.pallas import tpu as pltpu
from jax.sharding import PartitionSpec as P

HEADS = 25
HEAD_DIM = 64
EPS = 1e-05
LOG2E = 1.4426950408889634
NEG = -1e30
RING = (0, 2, 4, 6, 7, 5, 3, 1)

def fwd_kernel(heads, blk, n_blk, info_ref, blocks_ref, q_ref, k_ref, v_ref, o_ref, ot_ref, lse_ref, vt_ref):
    bound = info_ref[0]
    scale = LOG2E * 0.125
    span = 2 * 64
    vt_ref[...] = v_ref[...].T
    lane = lax.broadcasted_iota(jnp.int32, (blk, span), 1)
    masks = [lane < 64, lane >= 64]

    def rows(step, carry):
        i = blocks_ref[step]
        q0 = pl.multiple_of(i * blk, blk)
        q = q_ref[pl.ds(q0, blk), :]
        qs = [jnp.where(masks[h], q, jnp.zeros_like(q)) for h in range(heads)]
        qpos = q0 + lax.broadcasted_iota(jnp.int32, (1, blk), 1)
        lo = jnp.where(qpos < bound, 0, bound)
        first = jnp.where(q0 < bound, 0, bound // blk)

        def tile(j, state, masked):
            k0 = pl.multiple_of(j * blk, blk)
            k = k_ref[pl.ds(k0, blk), :]
            vt = vt_ref[:, pl.ds(k0, blk)]
            if masked:
                kpos = k0 + lax.broadcasted_iota(jnp.int32, (blk, 1), 0)
                allowed = (kpos <= qpos) & (kpos >= lo)
            out = []
            for h in range(heads):
                m, l, acc = state[h]
                s = lax.dot_general(k, qs[h], (((1,), (1,)), ((), ())), preferred_element_type=jnp.float32) * scale
                if masked:
                    s = jnp.where(allowed, s, NEG)
                new = jnp.maximum(m, jnp.max(s, axis=0, keepdims=True))
                p = jnp.exp2(s - new)
                if masked:
                    p = jnp.where(allowed, p, 0.0)
                alpha = jnp.exp2(m - new)
                l = l * alpha + jnp.sum(p, axis=0, keepdims=True)
                pv = lax.dot_general(vt[64 * h:64 * h + 64], p.astype(jnp.bfloat16), (((1,), (0,)), ((), ())), preferred_element_type=jnp.float32)
                out.append((new, l, acc * alpha + pv))
            return tuple(out)

        def step_fn(j, state):
            k0 = j * blk
            plain = (j < i) & ((q0 + blk <= bound) | (k0 >= bound))
            return lax.cond(plain, lambda s: tile(j, s, False), lambda s: tile(j, s, True), state)

        zero = tuple((jnp.full((1, blk), NEG, jnp.float32), jnp.zeros((1, blk), jnp.float32), jnp.zeros((64, blk), jnp.float32)) for _ in range(heads))
        state = lax.fori_loop(first, i + 1, step_fn, zero)
        outs = []
        for h in range(heads):
            m, l, acc = state[h]
            outs.append(acc * (1.0 / l))
            lse_ref[0, h:h + 1, pl.ds(q0, blk)] = m + jnp.log2(l)
        if heads == 1:
            outs.append(jnp.zeros((64, blk), jnp.float32))
        ot = jnp.concatenate(outs, axis=0)
        ot_ref[:, pl.ds(q0, blk)] = ot
        o_ref[pl.ds(q0, blk), :] = ot.T.astype(jnp.bfloat16)
        return carry

    if heads == 1:
        o_ref[...] = jnp.zeros_like(o_ref)
    lax.fori_loop(0, n_blk, rows, 0)

def attn_fwd(packed, info, blocks, heads, first_pair, pairs, width, blk, flops):
    size = packed.shape[0]
    at = width // 128
    spec = lambda base: pl.BlockSpec((size, 128), lambda p, *_: (0, base + first_pair + p))
    return pl.pallas_call(
        functools.partial(fwd_kernel, heads, blk, blocks.shape[0]),
        out_shape=(jax.ShapeDtypeStruct((size, 128 * pairs), jnp.bfloat16), jax.ShapeDtypeStruct((128 * pairs, size), jnp.float32), jax.ShapeDtypeStruct((pairs, 2, size), jnp.float32)),
        grid_spec=pltpu.PrefetchScalarGridSpec(
            num_scalar_prefetch=2, grid=(pairs,),
            in_specs=[spec(0), spec(at), spec(2 * at)],
            out_specs=[pl.BlockSpec((size, 128), lambda p, *_: (0, p)), pl.BlockSpec((128, size), lambda p, *_: (p, 0)), pl.BlockSpec((1, 2, size), lambda p, *_: (p, 0, 0))],
            scratch_shapes=[pltpu.VMEM((128, size), jnp.bfloat16)]),
        compiler_params=pltpu.CompilerParams(vmem_limit_bytes=48 * 2**20),
        cost_estimate=pl.CostEstimate(flops=flops, bytes_accessed=size * 128 * pairs * 12, transcendentals=0),
        name=f"attend_{heads}",
    )(info, blocks, packed, packed, packed)

def bwd_kernel(heads, blk, n_blk, info_ref, blocks_ref, q_ref, k_ref, v_ref, do_ref, ot_ref, lse_ref, dq_ref, dk_ref, dv_ref, kt_ref, dka_ref, dva_ref):
    bound = info_ref[0]
    scale = LOG2E * 0.125
    kt_ref[...] = k_ref[...].T
    dka_ref[...] = jnp.zeros_like(dka_ref)
    dva_ref[...] = jnp.zeros_like(dva_ref)
    if heads == 1:
        dq_ref[...] = jnp.zeros_like(dq_ref)
    lane = lax.broadcasted_iota(jnp.int32, (blk, 128), 1)
    masks = [lane < 64, lane >= 64]

    def rows(step, carry):
        i = blocks_ref[step]
        q0 = pl.multiple_of(i * blk, blk)
        q = q_ref[pl.ds(q0, blk), :]
        do = do_ref[pl.ds(q0, blk), :]
        qs = [jnp.where(masks[h], q, jnp.zeros_like(q)) for h in range(heads)]
        dos = [jnp.where(masks[h], do, jnp.zeros_like(do)) for h in range(heads)]
        prod = do.astype(jnp.float32).T * ot_ref[:, pl.ds(q0, blk)]
        deltas = [jnp.sum(prod[64 * h:64 * h + 64], axis=0, keepdims=True) for h in range(heads)]
        lses = [lse_ref[0, h:h + 1, pl.ds(q0, blk)] for h in range(heads)]
        qpos = q0 + lax.broadcasted_iota(jnp.int32, (1, blk), 1)
        lo = jnp.where(qpos < bound, 0, bound)
        first = jnp.where(q0 < bound, 0, bound // blk)

        def tile(j, state, masked):
            k0 = pl.multiple_of(j * blk, blk)
            k = k_ref[pl.ds(k0, blk), :]
            v = v_ref[pl.ds(k0, blk), :]
            kt = kt_ref[:, pl.ds(k0, blk)]
            if masked:
                kpos = k0 + lax.broadcasted_iota(jnp.int32, (blk, 1), 0)
                allowed = (kpos <= qpos) & (kpos >= lo)
            out = []
            dk = dka_ref[pl.ds(k0, blk), :]
            dv = dva_ref[pl.ds(k0, blk), :]
            for h in range(heads):
                s = lax.dot_general(k, qs[h], (((1,), (1,)), ((), ())), preferred_element_type=jnp.float32)
                p = jnp.exp2(s * scale - lses[h])
                if masked:
                    p = jnp.where(allowed, p, 0.0)
                dp = lax.dot_general(v, dos[h], (((1,), (1,)), ((), ())), preferred_element_type=jnp.float32)
                ds = (p * (dp - deltas[h])).astype(jnp.bfloat16)
                dv = dv + lax.dot_general(p.astype(jnp.bfloat16), dos[h], (((1,), (0,)), ((), ())), preferred_element_type=jnp.float32)
                dk = dk + lax.dot_general(ds, qs[h], (((1,), (0,)), ((), ())), preferred_element_type=jnp.float32)
                out.append(state[h] + lax.dot_general(kt[64 * h:64 * h + 64], ds, (((1,), (0,)), ((), ())), preferred_element_type=jnp.float32))
            dka_ref[pl.ds(k0, blk), :] = dk
            dva_ref[pl.ds(k0, blk), :] = dv
            return tuple(out)

        def step_fn(j, state):
            k0 = j * blk
            plain = (j < i) & ((q0 + blk <= bound) | (k0 >= bound))
            return lax.cond(plain, lambda s: tile(j, s, False), lambda s: tile(j, s, True), state)

        state = lax.fori_loop(first, i + 1, step_fn, tuple(jnp.zeros((64, blk), jnp.float32) for _ in range(heads)))
        outs = [s * 0.125 for s in state]
        if heads == 1:
            outs.append(jnp.zeros((64, blk), jnp.float32))
        dq_ref[pl.ds(q0, blk), :] = jnp.concatenate(outs, axis=0).T.astype(jnp.bfloat16)
        return carry

    lax.fori_loop(0, n_blk, rows, 0)
    dk_ref[...] = (dka_ref[...] * 0.125).astype(jnp.bfloat16)
    dv_ref[...] = dva_ref[...].astype(jnp.bfloat16)

def attn_bwd(packed, d_out, ot, lse, info, blocks, heads, first_pair, pairs, width, blk, flops):
    size = packed.shape[0]
    at = width // 128
    spec = lambda base: pl.BlockSpec((size, 128), lambda p, *_: (0, base + p))
    out = pl.BlockSpec((size, 128), lambda p, *_: (0, p))
    shape = jax.ShapeDtypeStruct((size, 128 * pairs), jnp.bfloat16)
    return pl.pallas_call(
        functools.partial(bwd_kernel, heads, blk, blocks.shape[0]),
        out_shape=(shape, shape, shape),
        grid_spec=pltpu.PrefetchScalarGridSpec(
            num_scalar_prefetch=2, grid=(pairs,),
            in_specs=[spec(first_pair), spec(at + first_pair), spec(2 * at + first_pair), spec(first_pair),
                      pl.BlockSpec((128, size), lambda p, *_: (p, 0)), pl.BlockSpec((1, 2, size), lambda p, *_: (p, 0, 0))],
            out_specs=[out, out, out],
            scratch_shapes=[pltpu.VMEM((128, size), jnp.bfloat16), pltpu.VMEM((size, 128), jnp.float32), pltpu.VMEM((size, 128), jnp.float32)]),
        compiler_params=pltpu.CompilerParams(vmem_limit_bytes=48 * 2**20),
        cost_estimate=pl.CostEstimate(flops=flops, bytes_accessed=size * 128 * pairs * 20, transcendentals=0),
        name=f"attend_back_{heads}",
    )(info, blocks, packed, packed, packed, d_out, ot, lse)


def layer_norm(values, gain_vec, shift_vec):
    row_mean = jnp.mean(values, axis=-1, keepdims=True)
    centred = values - row_mean
    spread = jnp.mean(centred * centred, axis=-1, keepdims=True)
    return centred * lax.rsqrt(spread + EPS) * gain_vec + shift_vec


def gelu_tanh(values):
    return (
        0.5
        * values
        * (1.0 + jnp.tanh(0.7978845608028654 * (values + 0.044715 * values * values * values)))
    )


def over_rows(left_side, right_side):
    return lax.dot_general(
        left_side, right_side, (((0,), (0,)), ((), ())), preferred_element_type=jnp.float32
    )


def by_rows(left_side, right_side):
    return lax.dot_general(
        left_side, right_side, (((1,), (1,)), ((), ())), preferred_element_type=jnp.float32
    )


def at(array, index, size, axis=0):
    return lax.dynamic_slice_in_dim(array, index, size, axis)


def put(buffer, piece, index):
    return lax.dynamic_update_slice_in_dim(buffer, piece[None], index, 0)


class Axes:
    def __init__(self, mesh):
        self.n_f = mesh.shape["fsdp"]
        self.n_c = mesh.shape["ctx"]
        self.f = lax.axis_index("fsdp")
        self.c = lax.axis_index("ctx")
        self.ring = RING if self.n_f == len(RING) else tuple(range(self.n_f))
        spot = [0] * self.n_f
        for place, index in enumerate(self.ring):
            spot[index] = place
        self.spot = jnp.array(spot, jnp.int32)[self.f]
        self.order = jnp.array(self.ring * 3, jnp.int32)
        n = self.n_f
        self.right = [(self.ring[p], self.ring[(p + 1) % n]) for p in range(n)]
        self.left = [(b, a) for a, b in self.right]

    def owner(self, shift):
        return self.order[self.spot + self.n_f + shift]

    def swap(self, array, bit, axis="ctx"):
        size = self.n_c if axis == "ctx" else self.n_f
        return lax.ppermute(array, axis, [(i, i ^ bit) for i in range(size)])

    def gather_f(self, piece):
        n, (rows, width) = self.n_f, piece.shape
        if n != len(RING):
            return lax.all_gather(piece, "fsdp", axis=0, tiled=True)
        cut = (rows // 2 + 7) // 8 * 8
        buffer = put(jnp.zeros((n, rows, width), piece.dtype), piece, self.f)
        right = left = piece
        for step in range(1, n // 2):
            right = lax.ppermute(right, "fsdp", self.right)
            left = lax.ppermute(left, "fsdp", self.left)
            buffer = put(put(buffer, right, self.owner(-step)), left, self.owner(step))
        top = lax.ppermute(right[:cut], "fsdp", self.right)
        low = lax.ppermute(left[cut:], "fsdp", self.left)
        far = self.owner(n // 2)
        buffer = lax.dynamic_update_slice(buffer, top[None], (far, 0, 0))
        buffer = lax.dynamic_update_slice(buffer, low[None], (far, cut, 0))
        return buffer.reshape(n * rows, width)

    def scatter_f(self, parts):
        n, width = self.n_f, parts.shape[1]
        rows = parts.shape[0] // n
        if n != len(RING):
            return lax.psum_scatter(parts, "fsdp", scatter_dimension=0, tiled=True).astype(jnp.float32)
        parts = parts.reshape(n, rows, width)
        cut = (rows // 2 + 7) // 8 * 8
        own = lambda shift: at(parts, self.owner(shift), 1)[0].astype(jnp.float32)
        far = at(parts, self.owner(n // 2), 1)[0]
        right = lax.ppermute(far[:cut], "fsdp", self.right)
        left = lax.ppermute(far[cut:], "fsdp", self.left)
        for step in range(n // 2 - 1, 0, -1):
            mine, yours = own(step), own(-step)
            if step == n // 2 - 1:
                mine = jnp.concatenate([mine[:cut] + right.astype(jnp.float32), mine[cut:]], axis=0)
                yours = jnp.concatenate([yours[:cut], yours[cut:] + left.astype(jnp.float32)], axis=0)
            else:
                mine = mine + right.astype(jnp.float32)
                yours = yours + left.astype(jnp.float32)
            right = lax.ppermute(mine.astype(jnp.bfloat16), "fsdp", self.right)
            left = lax.ppermute(yours.astype(jnp.bfloat16), "fsdp", self.left)
        return own(0) + right.astype(jnp.float32) + left.astype(jnp.float32)

    def gather_c(self, piece):
        across = self.swap(piece, 2)
        beside = self.swap(piece, 1)
        corner = self.swap(across, 1)
        buffer = put(jnp.zeros((self.n_c,) + piece.shape, piece.dtype), piece, self.c)
        buffer = put(buffer, beside, self.c ^ 1)
        buffer = put(buffer, across, self.c ^ 2)
        return put(buffer, corner, self.c ^ 3)

    def scatter_c(self, parts):
        away, home = self.c ^ 2, self.c
        take = lambda index: at(parts, index, 1)[0]
        far = self.swap(take(away ^ 1).astype(jnp.bfloat16), 1)
        far = take(away).astype(jnp.float32) + far.astype(jnp.float32)
        far = self.swap(far.astype(jnp.bfloat16), 2)
        near = self.swap(take(home ^ 1).astype(jnp.bfloat16), 1)
        return take(home).astype(jnp.float32) + near.astype(jnp.float32) + far.astype(jnp.float32)

    def exchange_c(self, make):
        mine = make(self.c)
        buffer = put(jnp.zeros((self.n_c,) + mine.shape, mine.dtype), mine, self.c)
        for bit in range(1, self.n_c):
            buffer = put(buffer, self.swap(make(self.c ^ bit), bit), self.c ^ bit)
        return buffer

    def total(self, array, axis):
        size = self.n_c if axis == "ctx" else self.n_f
        bit = 1
        while bit < size:
            array = array + self.swap(array, bit, axis)
            bit *= 2
        return array


def shards(mesh, tokens, segments, ln_gains, shifts, w_qkv, w_proj, w_fc, fc_bias, w_out, cotangent):
    ax = Axes(mesh)
    n_c, n_f, c, f = ax.n_c, ax.n_f, ax.c, ax.f
    rows, dim = tokens.shape
    shard = w_qkv.shape[0]
    hidden_units = w_fc.shape[1]
    size = rows * n_c
    own = HEADS // n_c * HEAD_DIM
    rest = dim - own * n_c
    both = own + rest
    width = (both + 127) // 128 * 128
    pad = width - both
    f32 = jnp.float32
    low = jnp.bfloat16

    def columns(array, base):
        return [at(array, base + own * c, own, 1), array[:, base + own * n_c : base + dim]]

    def blank(like, count):
        return jnp.zeros((like.shape[0], count), like.dtype)

    quarter_bias = at(fc_bias.reshape(n_c, shard), c, 1).reshape(shard, 1)
    extras = [ln_gains, shifts, quarter_bias]
    extra_count = 2 + 6 + 1
    piece = jnp.concatenate(
        columns(w_qkv, 0)
        + extras
        + [blank(w_qkv, pad - extra_count)]
        + columns(w_qkv, dim)
        + [blank(w_qkv, pad)]
        + columns(w_qkv, 2 * dim)
        + [blank(w_qkv, pad)],
        axis=1,
    )
    wqkv = ax.gather_f(piece)
    tokens_all = ax.gather_c(tokens).reshape(size, dim)
    bound = ax.total(jnp.sum((segments == 0).astype(jnp.int32)).reshape(1), "ctx")

    proj_piece = at(w_proj, own * c, both, 1)
    wproj = ax.gather_c(ax.gather_f(proj_piece))
    wproj = jnp.concatenate([wproj[i, :, :own] for i in range(n_c - 1)] + [wproj[n_c - 1]], axis=1)
    fc_piece = at(w_fc.reshape(shard, n_f, n_c, shard), c, 1, 2).reshape(shard, n_f * shard)
    wfc = ax.gather_f(fc_piece)
    wout = ax.gather_f(at(w_out, shard * c, shard))
    cot_all = ax.gather_c(cotangent).reshape(size, dim)

    vectors = wqkv[:, both : both + extra_count].astype(f32).T
    gain_one, gain_two, shift_one, bias_q, bias_v, bias_o, shift_two, bias_out, bias_fc = (
        vectors[i] for i in range(extra_count)
    )

    def spread(vector):
        return jnp.concatenate(columns(vector[None], 0) + [jnp.zeros((1, pad), f32)], axis=1)

    bias_packed = jnp.concatenate([spread(bias_q), jnp.zeros((1, width), f32), spread(bias_v)], axis=1)

    normed = layer_norm(tokens_all.astype(f32), gain_one, shift_one).astype(low)
    packed = (jnp.dot(normed, wqkv, preferred_element_type=f32) + bias_packed).astype(low)

    block = size // 4
    small = size // (2 * n_c)
    all_blocks = jnp.arange(size // block, dtype=jnp.int32)
    my_blocks = jnp.stack([c, 2 * n_c - 1 - c]).astype(jnp.int32)
    pairs = own // 128
    work = 2 * size * size // 2 * 128
    mixed_a, trans_a, lse_a = attn_fwd(packed, bound, all_blocks, 2, 0, pairs, width, block, 4 * pairs * work)
    mixed_b, trans_b, lse_b = attn_fwd(packed, bound, my_blocks, 1, pairs, 1, width, small, work // 2)

    def mixed_piece(index):
        return jnp.concatenate([at(mixed_a, index * rows, rows), at(mixed_b, index * rows, rows)[:, :rest]], axis=1)

    got = ax.exchange_c(mixed_piece)
    last = sum(got[i, :, own:].astype(f32) for i in range(n_c)).astype(low)
    mixed = jnp.concatenate([got[i, :, :own] for i in range(n_c)] + [last], axis=1)

    inputs = tokens.astype(f32)
    hidden = inputs + jnp.dot(mixed, wproj, preferred_element_type=f32) + bias_o
    normed_two = layer_norm(hidden, gain_two, shift_two).astype(low)
    two_all = ax.gather_c(normed_two).reshape(size, dim)

    d_active = by_rows(cot_all, wout)
    pre_act = jnp.dot(two_all, wfc, preferred_element_type=f32) + bias_fc
    active, gelu_back = jax.vjp(gelu_tanh, pre_act)
    active = active.astype(low)
    d_pre = gelu_back(d_active)[0].astype(low)

    d_two = ax.scatter_c(by_rows(d_pre, wfc).reshape(n_c, rows, dim))
    part = jnp.dot(active, wout, preferred_element_type=f32).reshape(n_c, rows, dim)
    result = hidden + ax.scatter_c(part) + bias_out
    grad_fc = ax.scatter_f(over_rows(two_all, d_pre).astype(low))
    grad_out = ax.scatter_f(over_rows(active, cot_all).astype(low))
    grad_fc_bias = jnp.sum(d_pre.astype(f32), axis=0)

    upstream = cotangent.astype(f32)
    d_hidden_norm, grad_gain_two, grad_shift_two = jax.vjp(layer_norm, hidden, gain_two, shift_two)[1](d_two)
    d_hidden = upstream + d_hidden_norm
    d_branch = d_hidden.astype(low)
    d_mixed = by_rows(d_branch, wproj).astype(low)

    def d_mixed_piece(index):
        return jnp.concatenate(
            [at(d_mixed, own * index, own, 1), d_mixed[:, own * n_c :], blank(d_mixed, pad)], axis=1
        )

    d_heads = ax.exchange_c(d_mixed_piece).reshape(size, width)
    grad_proj = over_rows(mixed, d_branch)
    grad_proj = jnp.stack([grad_proj[:, own * i : own * i + both] for i in range(n_c)])
    grad_proj = ax.scatter_f(ax.scatter_c(grad_proj).astype(low))

    back_a = attn_bwd(packed, d_heads, trans_a, lse_a, bound, all_blocks, 2, 0, pairs, width, block, 10 * pairs * work)
    back_b = attn_bwd(packed, d_heads, trans_b, lse_b, bound, my_blocks, 1, pairs, 1, width, small, 5 * work // 4)
    d_packed = jnp.concatenate([piece for pair in zip(back_a, back_b) for piece in pair], axis=1)

    grad_qkv = ax.scatter_f(over_rows(normed, d_packed).astype(low))
    d_normed = ax.scatter_c(by_rows(d_packed, wqkv).reshape(n_c, rows, dim))
    d_inputs_norm, grad_gain_one, grad_shift_one = jax.vjp(layer_norm, inputs, gain_one, shift_one)[1](d_normed)
    grad_tokens = d_hidden + d_inputs_norm

    bias_sums = jnp.sum(d_packed.astype(f32), axis=0, keepdims=True)

    def collect(base):
        whole = jnp.concatenate([jnp.zeros((1, own * n_c), f32), bias_sums[:, base + own : base + both]], axis=1)
        return lax.dynamic_update_slice(whole, bias_sums[:, base : base + own], (0, own * c))[0]

    sums = jnp.stack(
        [
            grad_gain_one,
            grad_gain_two,
            grad_shift_one,
            collect(0),
            collect(2 * width),
            jnp.sum(d_branch.astype(f32), axis=0),
            grad_shift_two,
            jnp.sum(upstream, axis=0),
        ]
    )
    sums = ax.total(ax.total(sums, "ctx"), "fsdp")
    sums = at(sums, shard * f, shard, 1).T
    bias_part = at(ax.total(grad_fc_bias.reshape(n_f, shard), "fsdp"), f, 1)[0]
    bias_parts = ax.gather_c(bias_part).reshape(-1)

    def join(parts):
        got = parts.astype(f32)
        return [got[i, :, :own] for i in range(n_c)] + [sum(got[i, :, own:both] for i in range(n_c))]

    qkv_parts = ax.gather_c(grad_qkv.astype(low))
    grad_qkv = jnp.concatenate(
        [column for i in range(3) for column in join(qkv_parts[:, :, i * width : (i + 1) * width])], axis=1
    )
    proj_parts = ax.gather_c(grad_proj.astype(low)).astype(f32)
    grad_proj = jnp.concatenate([proj_parts[i, :, :own] for i in range(n_c - 1)] + [proj_parts[n_c - 1]], axis=1)
    fc_parts = ax.gather_c(grad_fc.astype(low)).reshape(n_c, shard, n_f, shard)
    grad_fc = fc_parts.transpose(1, 2, 0, 3).reshape(shard, hidden_units).astype(f32)
    grad_out = ax.gather_c(grad_out.astype(low)).reshape(n_c * shard, dim).astype(f32)
    return (
        result,
        grad_tokens,
        sums[:, :2],
        sums[:, 2:],
        grad_qkv,
        grad_proj,
        grad_fc,
        bias_parts,
        grad_out,
    )


def solution(mesh):
    return jax.shard_map(
        functools.partial(shards, mesh),
        mesh=mesh,
        in_specs=(
            P(("fsdp", "ctx"), None),
            P("fsdp", "ctx"),
            P("fsdp", None),
            P("fsdp", None),
            P("fsdp", None),
            P("fsdp", None),
            P("fsdp", None),
            P("fsdp"),
            P("fsdp", None),
            P(("fsdp", "ctx"), None),
        ),
        out_specs=(
            P(("fsdp", "ctx"), None),
            P(("fsdp", "ctx"), None),
            P("fsdp", None),
            P("fsdp", None),
            P("fsdp", None),
            P("fsdp", None),
            P("fsdp", None),
            P("fsdp"),
            P("fsdp", None),
        ),
        check_vma=False,
    )
```
